128 devices in a mesh: chain: 8 (over y, core), col: 16 (over z, x).
Axes of the slice: x: 4, y: 4, z: 4, core: 2. Of those that a mesh axis runs over, the one named last changes fastest.
Arguments:
- sources: float32 [8, 64, 64, 128], P('chain', 'col'), may hold values from -6 to 6
- diag_inverse: float32 [8, 64, 128, 128], P('chain', 'col')
- factor_tiles: float32 [8, 1504, 128, 128], P('chain', 'col'), may hold values from -0.109375 to 0.109375
- tile_rows: int32 [8, 1504], P('chain', 'col'), may hold values from 0 to 63
- tile_cols: int32 [8, 1504], P('chain', 'col'), may hold values from 0 to 63, as said below
Outputs:
- solved: float32 [8, 64, 64, 128], P('chain', 'col')
- leaving: float32 [8, 64, 64, 128], P('chain', 'col')
The draws below stay inside these ranges and needn't reach their ends.
Inputs may be any that keep to these rules, and one draw needn't show every extreme that they name: `tile_cols`: entries 94 * c to 94 * (c + 1) - 1 of a group name tile columns 4 * c to 4 * (c + 1) - 1.
All inputs are finite; a program needn't handle non-finite values.
Results may differ from the reference program's by a relative error of at most 0.00018.
Values sent between devices are 32-bit elements; how exact they have to be, the bound alone decides.
No kernel may reach another device: no remote copies, remote signals or barrier semaphores. Data moves between devices by JAX's collectives and lax.ppermute only.
A program may use at most 64 MiB of HBM per device.

```python
import jax
import jax.numpy as jnp
from jax import lax

TILE = 128
SRC = 64
TPD = 4
NOFF = 94
GROUPS = 8
NT = 64
OFFALL = 1504
FAN = 3008


def draw_diag_inverse(key, part):
    first = jax.random.fold_in(key, 11)
    second = jax.random.fold_in(key, 12)
    diag_values = jnp.exp(jax.random.uniform(first, (GROUPS, NT, TILE), jnp.float32, jnp.log(0.5), jnp.log(2.0)))
    off_part = jax.random.normal(second, (GROUPS, NT, TILE, TILE), jnp.float32) * (0.35 / jnp.sqrt(TILE * 1.0))
    eye_mat = jnp.eye(TILE, dtype=jnp.float32)
    matrix = off_part + diag_values[..., None] * eye_mat
    return matrix


def draw_tile_cols(key, part):
    picks = jax.random.randint(jax.random.fold_in(key, 21), (GROUPS, OFFALL), 0, TPD)
    blocks = jnp.arange(OFFALL, dtype=jnp.int32) // NOFF
    return (blocks[None, :] * TPD + picks).astype(jnp.int32)


def with_ends(drawn, key, smallest, high):
    index_at = [jax.random.randint(jax.random.fold_in(key, axis), (), 0, length) for axis, length in enumerate(drawn.shape)]
    longest = drawn.shape.index(max(drawn.shape))
    beside = index_at[:longest] + [(index_at[longest] + 1) % drawn.shape[longest]] + index_at[longest + 1:]
    return drawn.at[tuple(index_at)].set(smallest).at[tuple(beside)].set(high)


def shard_levels(stream_key, shape, split, smallest, high):
    loudness = 1.0
    for axis_at, blocks in split:
        draws = jax.random.uniform(jax.random.fold_in(jax.random.fold_in(stream_key, 6), axis_at), (blocks,), jnp.float32, smallest / len(split), high / len(split))
        loudness = loudness * jnp.repeat(jnp.exp(draws), shape[axis_at] // blocks).reshape((-1,) + (1,) * (len(shape) - 1 - axis_at))
    return loudness


def centred(rng, extent, deviation, most, pieces=(), kind=jnp.bfloat16):
    gain = shard_levels(rng, extent, pieces, -0.22, 0.18) if pieces else 1.0
    drawn = jax.random.normal(rng, extent, jnp.float32) * deviation * gain
    return jnp.minimum(jnp.maximum(drawn, -most), most).astype(kind)


def setup_inputs(seed: int = 0) -> dict:
    key_list = jax.random.split(jax.random.key(seed), 6)
    sources = centred(key_list[0], (GROUPS, NT, SRC, TILE), 1.0, 6.0, ((0, 8), (1, 16)), jnp.float32)
    diag_inverse = draw_diag_inverse(jax.random.fold_in(key_list[5], 71), 0)
    factor_tiles = centred(key_list[2], (GROUPS, OFFALL, TILE, TILE), FAN ** -0.5, 0.109375, ((0, 8), (1, 16)), jnp.float32)
    tile_rows = with_ends(jax.random.randint(key_list[3], (GROUPS, OFFALL), 0, NT), jax.random.fold_in(key_list[3], 1), 0, NT - 1).astype(jnp.int32)
    tile_cols = draw_tile_cols(jax.random.fold_in(key_list[5], 71), 0)
    return {"sources": sources, "diag_inverse": diag_inverse, "factor_tiles": factor_tiles, "tile_rows": tile_rows, "tile_cols": tile_cols}


def reference(sources, diag_inverse, factor_tiles, tile_rows, tile_cols):
    highest = lax.Precision.HIGHEST
    inbound = jnp.zeros((NT, SRC, TILE), jnp.float32)
    solved_list = []
    leaving_list = []
    for group in range(GROUPS):
        right_side = sources[group] - inbound
        current = jnp.einsum("trc,tsc->tsr", diag_inverse[group], right_side, precision=highest)
        picked = jnp.take(current, tile_cols[group].astype(jnp.int32), axis=0)
        products = jnp.einsum("krc,ksc->ksr", factor_tiles[group], picked, precision=highest)
        onehot = (tile_rows[group][:, None] == jnp.arange(NT, dtype=jnp.int32)[None, :]).astype(jnp.float32)
        inbound = jnp.einsum("kt,ksr->tsr", onehot, products, precision=highest)
        solved_list.append(current)
        leaving_list.append(inbound)
    return jnp.stack(solved_list), jnp.stack(leaving_list)
```

```python
import functools

import jax
import jax.numpy as jnp
from jax import lax
from jax.experimental import pallas as pl
from jax.experimental.pallas import tpu as pltpu
from jax.sharding import PartitionSpec as P

BF = jnp.bfloat16
F32 = jnp.float32
VMEM = pl.BlockSpec(memory_space=pltpu.VMEM)
SMEM = pl.BlockSpec(memory_space=pltpu.SMEM)


def split(x):
    high = x.astype(BF)
    return high, (x - high.astype(F32)).astype(BF)


def left_side(x):
    high, low = split(x)
    return jnp.concatenate(
        [
            jnp.concatenate([high, high], 1),
            jnp.concatenate([low, jnp.zeros_like(low)], 1),
        ],
        0,
    )


def product(left, right):
    both = jnp.dot(left, right, preferred_element_type=F32)
    half = both.shape[0] // 2
    return both[:half] + both[half:]


def prepare_body(first, tile_ref, *refs):
    out_ref = refs[-1]

    @pl.loop(0, tile_ref.shape[0], unroll=2)
    def _(i):
        high, low = split(tile_ref[i].T)
        size = high.shape[0]
        out_ref[first + i, :size] = high
        out_ref[first + i, size:] = low


def prepare(tiles, into=None):
    count, size = tiles.shape[0], tiles.shape[1]
    first = 0 if into is None else count
    return pl.pallas_call(
        functools.partial(prepare_body, first),
        out_shape=jax.ShapeDtypeStruct((2 * count, 2 * size, size), BF),
        in_specs=[VMEM] if into is None else [VMEM, VMEM],
        out_specs=VMEM,
        input_output_aliases={} if into is None else {1: 0},
        compiler_params=pltpu.CompilerParams(vmem_limit_bytes=24 << 20),
        name="prepare",
    )(*((tiles,) if into is None else (tiles, into)))


def stage_body(place, rows, cols, arrived, source, inverse, factor, sums, solved, inbound, current):
    slot = place[0]
    live = place[1]
    tiles = factor.shape[0] // 2
    columns = source.shape[0]
    sums[...] = jnp.zeros_like(sums)
    for t in range(columns):
        total = arrived[0, t]
        for j in range(1, arrived.shape[0]):
            total = total + arrived[j, t]
        total = jnp.where(live > 0, total, jnp.zeros_like(total))
        inbound[t] = total
        here = product(left_side(source[t] - total), inverse[slot * columns + t])
        solved[t] = here
        current[t] = left_side(here)
    base = slot * tiles
    for k in range(tiles):
        sums[rows[k]] += product(current[cols[k]], factor[base + k])


def stage(place, rows, cols, arrived, source, inverse, factor, tile_rows):
    columns, width, size = source.shape
    small = jax.ShapeDtypeStruct(source.shape, F32)
    return pl.pallas_call(
        stage_body,
        out_shape=(jax.ShapeDtypeStruct((tile_rows, width, size), F32), small, small),
        in_specs=[SMEM, SMEM, SMEM, VMEM, VMEM, VMEM, VMEM],
        out_specs=[VMEM, VMEM, VMEM],
        scratch_shapes=[pltpu.VMEM((columns, 2 * width, 2 * size), BF)],
        compiler_params=pltpu.CompilerParams(vmem_limit_bytes=6 << 20),
        name="stage",
    )(place, rows, cols, arrived, source, inverse, factor)


def local(sources, diag_inverse, factor_tiles, tile_rows, tile_cols):
    group = lax.axis_index("chain")
    groups = lax.axis_size("chain")
    peers = lax.axis_size("col")
    core = group % 2
    plane = group // 2
    columns = sources.shape[1]
    width = sources.shape[2] // 2

    def swap(x):
        return lax.ppermute(x, "chain", [(i, i ^ 1) for i in range(groups)])

    own_factor = factor_tiles[0]
    other_factor = swap(own_factor)
    own_inverse = diag_inverse[0]
    other_inverse = swap(own_inverse)
    own_rows = tile_rows[0]
    own_cols = tile_cols[0] - lax.axis_index("col") * columns
    own_index = jnp.concatenate([own_rows, own_cols])
    other_index = swap(own_index)
    kept = lax.dynamic_slice_in_dim(sources[0], core * width, width, 1)
    given = lax.dynamic_slice_in_dim(sources[0], (1 - core) * width, width, 1)
    taken = swap(given)

    factor = prepare(other_factor, prepare(own_factor))
    inverse = prepare(other_inverse, prepare(own_inverse))
    count = own_rows.shape[0]
    first = core == 0
    source = [jnp.where(first, kept, taken), jnp.where(first, taken, kept)]
    index = [jnp.where(first, own_index, other_index), jnp.where(first, other_index, own_index)]
    rows = [i[:count] for i in index]
    cols = [i[count:] for i in index]
    slot = [core, 1 - core]
    live = jnp.where(plane > 0, 1, 0)
    place = [jnp.stack([slot[0], live]), jnp.stack([slot[1], jnp.ones_like(live)])]

    def exchange(x):
        return lax.all_to_all(x.reshape((peers, columns) + x.shape[1:]), "col", 0, 0)

    arrived = jnp.zeros((1, columns, width, sources.shape[3]), F32)
    planes = groups // 2
    for sweep in range(planes):
        sums, solved_even, _ = stage(place[0], rows[0], cols[0], arrived, source[0], inverse, factor, peers * columns)
        sums, solved_odd, leaving_even = stage(
            place[1], rows[1], cols[1], exchange(sums), source[1], inverse, factor, peers * columns
        )
        leaving_odd = jnp.sum(exchange(sums), 0)
        if sweep < planes - 1:
            arrived = lax.ppermute(leaving_odd, "chain", [(i, (i + 2) % groups) for i in range(groups)])[None]

    even = jnp.stack([solved_even, leaving_even])
    odd = jnp.stack([solved_odd, leaving_odd])
    mine = jnp.where(first, even, odd)
    partner = swap(jnp.where(first, odd, even))
    whole = jnp.where(first, jnp.concatenate([mine, partner], 2), jnp.concatenate([partner, mine], 2))
    return (whole[0][None], whole[1][None])


def solution(mesh):
    return jax.shard_map(
        local,
        mesh=mesh,
        in_specs=(
            P("chain", "col", None, None),
            P("chain", "col", None, None),
            P("chain", "col", None, None),
            P("chain", "col"),
            P("chain", "col"),
        ),
        out_specs=(P("chain", "col", None, None), P("chain", "col", None, None)),
        check_vma=False,
    )
```

```python
import functools

import jax
import jax.numpy as jnp
from jax import lax
from jax.experimental import pallas as pl
from jax.experimental.pallas import tpu as pltpu
from jax.sharding import PartitionSpec as P

BF = jnp.bfloat16
F32 = jnp.float32
VMEM = pl.BlockSpec(memory_space=pltpu.VMEM)
SMEM = pl.BlockSpec(memory_space=pltpu.SMEM)


def split(x):
    high = x.astype(BF)
    return high, (x - high.astype(F32)).astype(BF)


def left_side(x):
    high, low = split(x)
    return jnp.concatenate(
        [
            jnp.concatenate([high, high], 1),
            jnp.concatenate([low, jnp.zeros_like(low)], 1),
        ],
        0,
    )


def product(left, right):
    both = jnp.dot(left, right, preferred_element_type=F32)
    half = both.shape[0] // 2
    return both[:half] + both[half:]


def prepare_tile(tile, out_ref, at):
    high, low = split(tile.T)
    size = high.shape[0]
    out_ref[at, :size] = high
    out_ref[at, size:] = low


def prepare_body(first, tile_ref, *refs):
    out_ref = refs[-1]

    @pl.loop(0, tile_ref.shape[0], unroll=8)
    def _(i):
        prepare_tile(tile_ref[i], out_ref, first + i)


def prepare(tiles, other_tiles):
    count, size = tiles.shape[0], tiles.shape[1]
    both = jax.ShapeDtypeStruct((2 * count, 2 * size, size), BF)
    grant = pltpu.CompilerParams(vmem_limit_bytes=20 << 20)
    half = pl.pallas_call(
        functools.partial(prepare_body, 0),
        out_shape=both,
        in_specs=[VMEM],
        out_specs=VMEM,
        compiler_params=grant,
        name="prepare_first",
    )(tiles)
    return pl.pallas_call(
        functools.partial(prepare_body, count),
        out_shape=both,
        in_specs=[VMEM, VMEM],
        out_specs=VMEM,
        input_output_aliases={1: 0},
        compiler_params=grant,
        name="prepare_second",
    )(other_tiles, half)


def gather_sum_body(arrived, total):
    for t in range(arrived.shape[1]):
        value = arrived[0, t]
        for j in range(1, arrived.shape[0]):
            value = value + arrived[j, t]
        total[t] = value


def gather_sum(arrived):
    return pl.pallas_call(
        gather_sum_body,
        out_shape=jax.ShapeDtypeStruct(arrived.shape[1:], F32),
        in_specs=[VMEM],
        out_specs=VMEM,
        compiler_params=pltpu.CompilerParams(vmem_limit_bytes=4 << 20),
        name="gather_sum",
    )(arrived)


def stage_body(
    place, rows, cols, other_rows, other_cols, arrived, source, other_source, inverse, factor, sums, solved, inbound, current
):
    slot, live, first, shift = place[0], place[1], place[2], place[3]
    tiles = factor.shape[0] // 2
    columns, width = inbound.shape[0], inbound.shape[1]
    here = pl.ds(pl.multiple_of(first, width), width)
    sums[...] = jnp.zeros_like(sums)
    for t in range(columns):
        total = arrived[0, t]
        for j in range(1, arrived.shape[0]):
            total = total + arrived[j, t]
        total = jnp.where(live > 0, total, jnp.zeros_like(total))
        inbound[t] = total
        right = jnp.where(slot > 0, other_source[0, t, here], source[0, t, here]) - total
        value = product(left_side(right), inverse[slot * columns + t])
        solved[t] = value
        current[t] = left_side(value)
    base = slot * tiles
    for k in range(tiles):
        row = jnp.where(slot > 0, other_rows[0, k], rows[0, k])
        col = jnp.where(slot > 0, other_cols[0, k], cols[0, k]) - shift
        sums[row] += product(current[col], factor[base + k])


def stage(place, tables, arrived, inputs, tile_rows):
    small = jax.ShapeDtypeStruct(arrived.shape[1:], F32)
    columns, width, size = small.shape
    return pl.pallas_call(
        stage_body,
        out_shape=(jax.ShapeDtypeStruct((tile_rows, width, size), F32), small, small),
        in_specs=[SMEM] * 5 + [VMEM] * 5,
        out_specs=[VMEM, VMEM, VMEM],
        scratch_shapes=[pltpu.VMEM((columns, 2 * width, 2 * size), BF)],
        compiler_params=pltpu.CompilerParams(vmem_limit_bytes=6 << 20),
        name="stage",
    )(place, *tables, arrived, *inputs)


def local(sources, diag_inverse, factor_tiles, tile_rows, tile_cols):
    group = lax.axis_index("chain")
    groups = lax.axis_size("chain")
    peers = lax.axis_size("col")
    core = lax.rem(group, 2)
    columns = sources.shape[1]
    width = sources.shape[2] // 2

    def swap(x):
        return lax.ppermute(x, "chain", [(i, i ^ 1) for i in range(groups)])

    def exchange(x):
        return lax.all_to_all(x.reshape((peers, columns) + x.shape[1:]), "col", 0, 0)

    lowest = core * width
    shift = lax.axis_index("col") * columns
    live = jnp.where(group > 1, 1, 0)
    place = [jnp.stack([core, live, lowest, shift]), jnp.stack([1 - core, jnp.ones_like(live), lowest, shift])]
    place, factor_tiles = lax.optimization_barrier((place, factor_tiles))

    other_factor = swap(factor_tiles[0])
    other_inverse = swap(diag_inverse[0])
    tables = (tile_rows, tile_cols, swap(tile_rows), swap(tile_cols))
    inputs = (
        sources,
        swap(sources),
        prepare(diag_inverse[0], other_inverse),
        prepare(factor_tiles[0], other_factor),
    )

    arrived = jnp.zeros((1, columns, width, sources.shape[3]), F32)
    planes = groups // 2
    for sweep in range(planes):
        sums, solved_even, _ = stage(place[0], tables, arrived, inputs, peers * columns)
        sums, solved_odd, leaving_even = stage(place[1], tables, exchange(sums), inputs, peers * columns)
        leaving_odd = gather_sum(exchange(sums))
        if sweep < planes - 1:
            arrived = lax.ppermute(leaving_odd, "chain", [(i, (i + 2) % groups) for i in range(groups)])[None]

    first = core == 0
    even = jnp.stack([solved_even, leaving_even])
    odd = jnp.stack([solved_odd, leaving_odd])
    mine = jnp.where(first, even, odd)
    partner = swap(jnp.where(first, odd, even))
    whole = jnp.where(first, jnp.concatenate([mine, partner], 2), jnp.concatenate([partner, mine], 2))
    return (whole[0][None], whole[1][None])


def solution(mesh):
    return jax.shard_map(
        local,
        mesh=mesh,
        in_specs=(
            P("chain", "col", None, None),
            P("chain", "col", None, None),
            P("chain", "col", None, None),
            P("chain", "col"),
            P("chain", "col"),
        ),
        out_specs=(P("chain", "col", None, None), P("chain", "col", None, None)),
        check_vma=False,
    )
```

```python
import functools

import jax
import jax.numpy as jnp
from jax import lax
from jax.experimental import pallas as pl
from jax.experimental.pallas import tpu as pltpu
from jax.sharding import PartitionSpec as P

BF = jnp.bfloat16
F32 = jnp.float32
NONE, OLD, NEW = 0, 1, 2
PACE = 15
VMEM = pl.BlockSpec(memory_space=pltpu.VMEM)
SMEM = pl.BlockSpec(memory_space=pltpu.SMEM)


def split(x):
    high = x.astype(BF)
    return high, (x - high.astype(F32)).astype(BF)


def left_side(x):
    high, low = split(x)
    return jnp.concatenate(
        [
            jnp.concatenate([high, high], 1),
            jnp.concatenate([low, jnp.zeros_like(low)], 1),
        ],
        0,
    )


def product(left, right):
    both = jnp.dot(left, right, preferred_element_type=F32)
    half = both.shape[0] // 2
    return both[:half] + both[half:]


def prepare_tile(tile, out_ref, at):
    high, low = split(tile.T)
    size = high.shape[0]
    out_ref[at, :size] = high
    out_ref[at, size:] = low


def prepare_tiles(tile_ref, out_ref, first, count):
    @pl.loop(0, count, unroll=8)
    def _(i):
        prepare_tile(tile_ref[i], out_ref, first + i)


def prepare_own_body(tile_ref, inverse_ref, out_ref, out_inverse_ref):
    prepare_tiles(tile_ref, out_ref, 0, tile_ref.shape[0])
    prepare_tiles(inverse_ref, out_inverse_ref, 0, inverse_ref.shape[0])


def prepare_other_body(place, tile_ref, inverse_ref, held_ref, held_inverse_ref, out_ref, out_inverse_ref):
    count, columns = tile_ref.shape[0], inverse_ref.shape[0]
    prepare_tiles(tile_ref, out_ref, count, count)
    prepare_tiles(inverse_ref, out_inverse_ref, columns, columns)

    @pl.when(place[0] == 0)
    def _():
        prepare_tiles(tile_ref, out_ref, count, count * PACE // 16)


def prepare(place, own, own_inverse, other, other_inverse):
    count, size = own.shape[0], own.shape[1]
    columns = own_inverse.shape[0]
    shapes = (
        jax.ShapeDtypeStruct((2 * count, 2 * size, size), BF),
        jax.ShapeDtypeStruct((2 * columns, 2 * size, size), BF),
    )
    grant = pltpu.CompilerParams(vmem_limit_bytes=20 << 20)
    held = pl.pallas_call(
        prepare_own_body,
        out_shape=shapes,
        in_specs=[VMEM, VMEM],
        out_specs=(VMEM, VMEM),
        compiler_params=grant,
        name="prepare_own",
    )(own, own_inverse)
    return pl.pallas_call(
        prepare_other_body,
        out_shape=shapes,
        in_specs=[SMEM] + [VMEM] * 4,
        out_specs=(VMEM, VMEM),
        input_output_aliases={3: 0, 4: 1},
        compiler_params=grant,
        name="prepare_other",
    )(place, other, other_inverse, *held)


def gather_sum_body(arrived, total):
    for t in range(arrived.shape[1]):
        value = arrived[0, t]
        for j in range(1, arrived.shape[0]):
            value = value + arrived[j, t]
        total[t] = value


def gather_sum(arrived):
    return pl.pallas_call(
        gather_sum_body,
        out_shape=jax.ShapeDtypeStruct(arrived.shape[1:], F32),
        in_specs=[VMEM],
        out_specs=VMEM,
        compiler_params=pltpu.CompilerParams(vmem_limit_bytes=4 << 20),
        name="gather_sum",
    )(arrived)


def stage_body(
    place, rows, cols, other_rows, other_cols, arrived, before, source, other_source, inverse, factor, sums, solved, inbound, current
):
    slot, origin, first, shift = place[0], place[1], place[2], place[3]
    tiles = factor.shape[0] // 2
    columns, width = inbound.shape[0], inbound.shape[1]
    here = pl.ds(pl.multiple_of(first, width), width)
    sums[...] = jnp.zeros_like(sums)
    for t in range(columns):
        total = arrived[0, t]
        for j in range(1, arrived.shape[0]):
            total = total + arrived[j, t]
        if before is not None:
            total = jnp.where(origin == NEW, total, jnp.where(origin == OLD, before[0, t], jnp.zeros_like(total)))
        inbound[t] = total
        right = jnp.where(slot > 0, other_source[0, t, here], source[0, t, here]) - total
        value = product(left_side(right), inverse[slot * columns + t])
        solved[t] = value
        current[t] = left_side(value)
    base = slot * tiles
    for k in range(tiles):
        row = jnp.where(slot > 0, other_rows[0, k], rows[0, k])
        col = jnp.where(slot > 0, other_cols[0, k], cols[0, k]) - shift
        sums[row] += product(current[col], factor[base + k])


def stage(place, tables, arrived, before, inputs, tile_rows):
    body = stage_body
    if before is None:

        def body(*refs):
            stage_body(*refs[:6], None, *refs[6:])

    arrivals = (arrived,) if before is None else (arrived, before)
    small = jax.ShapeDtypeStruct(arrived.shape[1:], F32)
    columns, width, size = small.shape
    return pl.pallas_call(
        body,
        out_shape=(jax.ShapeDtypeStruct((tile_rows, width, size), F32), small, small),
        in_specs=[SMEM] * 5 + [VMEM] * (len(arrivals) + 4),
        out_specs=[VMEM, VMEM, VMEM],
        scratch_shapes=[pltpu.VMEM((columns, 2 * width, 2 * size), BF)],
        compiler_params=pltpu.CompilerParams(vmem_limit_bytes=6 << 20),
        name="stage",
    )(place, *tables, *arrivals, *inputs)


def local(sources, diag_inverse, factor_tiles, tile_rows, tile_cols):
    group = lax.axis_index("chain")
    groups = lax.axis_size("chain")
    peers = lax.axis_size("col")
    core = group % 2
    columns = sources.shape[1]
    width = sources.shape[2] // 2

    def swap(x):
        return lax.ppermute(x, "chain", [(i, i ^ 1) for i in range(groups)])

    def exchange(x):
        return lax.all_to_all(x.reshape((peers, columns) + x.shape[1:]), "col", 0, 0)

    lowest = core * width
    shift = lax.axis_index("col") * columns
    plane = group // 2
    origin = jnp.where(plane == 0, NONE, NEW)
    last = jnp.where(plane == 2, OLD, origin)
    place = [
        jnp.stack([core, origin, lowest, shift]),
        jnp.stack([core, last, lowest, shift]),
        jnp.stack([1 - core, origin, lowest, shift]),
    ]
    place, factor_tiles = lax.optimization_barrier((place, factor_tiles))

    other_inverse = swap(diag_inverse[0])
    tables = (tile_rows, tile_cols, swap(tile_rows), swap(tile_cols))
    other_sources = swap(sources)
    other_factor = swap(factor_tiles[0])
    factor, inverse = prepare(place[0], factor_tiles[0], diag_inverse[0], other_factor, other_inverse)
    inputs = (sources, other_sources, inverse, factor)

    trades = [{0: 1, 1: 0, 2: 3, 3: 2}, {0: 3, 1: 2, 2: 1, 3: 0}, {0: 1, 1: 0, 2: 3, 3: 2}]
    arrived = jnp.zeros((1, columns, width, sources.shape[3]), F32)
    before = arrived
    planes = groups // 2
    for sweep in range(planes):
        here = place[1] if sweep == planes - 1 else place[0]
        sums, solved_even, _ = stage(here, tables, arrived, before, inputs, peers * columns)
        sums, solved_odd, leaving_even = stage(place[2], tables, exchange(sums), None, inputs, peers * columns)
        leaving_odd = gather_sum(exchange(sums))
        if sweep < planes - 1:
            trade = trades[sweep]
            route = [(i, 2 * trade[i // 2] + i % 2) for i in range(groups)]
            before, arrived = arrived, lax.ppermute(leaving_odd, "chain", route)[None]

    first = core == 0
    even = jnp.stack([solved_even, leaving_even])
    odd = jnp.stack([solved_odd, leaving_odd])
    mine = jnp.where(first, even, odd)
    partner = swap(jnp.where(first, odd, even))
    whole = jnp.where(first, jnp.concatenate([mine, partner], 2), jnp.concatenate([partner, mine], 2))
    return (whole[0][None], whole[1][None])


def solution(mesh):
    return jax.shard_map(
        local,
        mesh=mesh,
        in_specs=(
            P("chain", "col", None, None),
            P("chain", "col", None, None),
            P("chain", "col", None, None),
            P("chain", "col"),
            P("chain", "col"),
        ),
        out_specs=(P("chain", "col", None, None), P("chain", "col", None, None)),
        check_vma=False,
    )
```

```python
import functools

import jax
import jax.numpy as jnp
from jax import lax
from jax.experimental import pallas as pl
from jax.experimental.pallas import tpu as pltpu
from jax.sharding import PartitionSpec as P

BF = jnp.bfloat16
F32 = jnp.float32
NONE, OLD, NEW = 0, 1, 2
LEAD, HOLD = 48, 50
VMEM = pl.BlockSpec(memory_space=pltpu.VMEM)
SMEM = pl.BlockSpec(memory_space=pltpu.SMEM)


def split(x):
    high = x.astype(BF)
    return high, (x - high.astype(F32)).astype(BF)


def left_side(x):
    high, low = split(x)
    return jnp.concatenate(
        [
            jnp.concatenate([high, high], 1),
            jnp.concatenate([low, jnp.zeros_like(low)], 1),
        ],
        0,
    )


def product(left, right):
    both = jnp.dot(left, right, preferred_element_type=F32)
    half = both.shape[0] // 2
    return both[:half] + both[half:]


def prepare_tile(tile, out_ref, at):
    high, low = split(tile.T)
    size = high.shape[0]
    out_ref[at, :size] = high
    out_ref[at, size:] = low


def prepare_tiles(tile_ref, out_ref, first, count):
    for i in range(count):
        prepare_tile(tile_ref[i], out_ref, first + i)


def prepare_own_body(tile_ref, inverse_ref, out_ref, out_inverse_ref):
    prepare_tiles(tile_ref, out_ref, 0, tile_ref.shape[0])
    prepare_tiles(inverse_ref, out_inverse_ref, 0, inverse_ref.shape[0])


def prepare_other_body(tile_ref, inverse_ref, held_ref, held_inverse_ref, out_ref, out_inverse_ref):
    count, columns = tile_ref.shape[0], inverse_ref.shape[0]
    prepare_tiles(tile_ref, out_ref, count, count)
    prepare_tiles(inverse_ref, out_inverse_ref, columns, columns)


def prepare(own, own_inverse, other, other_inverse):
    count, size = own.shape[0], own.shape[1]
    columns = own_inverse.shape[0]
    shapes = (
        jax.ShapeDtypeStruct((2 * count, 2 * size, size), BF),
        jax.ShapeDtypeStruct((2 * columns, 2 * size, size), BF),
    )
    grant = pltpu.CompilerParams(vmem_limit_bytes=20 << 20)
    held = pl.pallas_call(
        prepare_own_body,
        out_shape=shapes,
        in_specs=[VMEM, VMEM],
        out_specs=(VMEM, VMEM),
        compiler_params=grant,
        name="prepare_own",
    )(own, own_inverse)
    return pl.pallas_call(
        prepare_other_body,
        out_shape=shapes,
        in_specs=[VMEM] * 4,
        out_specs=(VMEM, VMEM),
        input_output_aliases={2: 0, 3: 1},
        compiler_params=grant,
        name="prepare_other",
    )(other, other_inverse, *held)


def gather_sum_body(arrived, total):
    for t in range(arrived.shape[1]):
        value = arrived[0, t]
        for j in range(1, arrived.shape[0]):
            value = value + arrived[j, t]
        total[t] = value


def gather_sum(arrived):
    return pl.pallas_call(
        gather_sum_body,
        out_shape=jax.ShapeDtypeStruct(arrived.shape[1:], F32),
        in_specs=[VMEM],
        out_specs=VMEM,
        compiler_params=pltpu.CompilerParams(vmem_limit_bytes=4 << 20),
        name="gather_sum",
    )(arrived)


def stage_body(
    place, rows, cols, other_rows, other_cols, arrived, before, source, other_source, inverse, factor, sums, solved, inbound, current
):
    slot, origin, first, shift = place[0], place[1], place[2], place[3]
    tiles = factor.shape[0] // 2
    columns, width = inbound.shape[0], inbound.shape[1]
    here = pl.ds(pl.multiple_of(first, width), width)

    @pl.loop(0, place[4])
    def _(_):
        sums[...] = jnp.zeros_like(sums)

    for t in range(columns):
        total = arrived[0, t]
        for j in range(1, arrived.shape[0]):
            total = total + arrived[j, t]
        if before is not None:
            total = jnp.where(origin == NEW, total, jnp.where(origin == OLD, before[0, t], jnp.zeros_like(total)))
        inbound[t] = total
        right = jnp.where(slot > 0, other_source[0, t, here], source[0, t, here]) - total
        value = product(left_side(right), inverse[slot * columns + t])
        solved[t] = value
        current[t] = left_side(value)
    base = slot * tiles
    for k in range(tiles):
        row = jnp.where(slot > 0, other_rows[0, k], rows[0, k])
        col = jnp.where(slot > 0, other_cols[0, k], cols[0, k]) - shift
        sums[row] += product(current[col], factor[base + k])


def stage(place, tables, arrived, before, inputs, tile_rows):
    body = stage_body
    if before is None:

        def body(*refs):
            stage_body(*refs[:6], None, *refs[6:])

    arrivals = (arrived,) if before is None else (arrived, before)
    small = jax.ShapeDtypeStruct(arrived.shape[1:], F32)
    columns, width, size = small.shape
    return pl.pallas_call(
        body,
        out_shape=(jax.ShapeDtypeStruct((tile_rows, width, size), F32), small, small),
        in_specs=[SMEM] * 5 + [VMEM] * (len(arrivals) + 4),
        out_specs=[VMEM, VMEM, VMEM],
        scratch_shapes=[pltpu.VMEM((columns, 2 * width, 2 * size), BF)],
        compiler_params=pltpu.CompilerParams(vmem_limit_bytes=6 << 20),
        name="stage",
    )(place, *tables, *arrivals, *inputs)


def local(sources, diag_inverse, factor_tiles, tile_rows, tile_cols):
    group = lax.axis_index("chain")
    groups = lax.axis_size("chain")
    peers = lax.axis_size("col")
    core = group % 2
    columns = sources.shape[1]
    width = sources.shape[2] // 2

    def swap(x):
        return lax.ppermute(x, "chain", [(i, i ^ 1) for i in range(groups)])

    def exchange(x):
        return lax.all_to_all(x.reshape((peers, columns) + x.shape[1:]), "col", 0, 0)

    lowest = core * width
    shift = lax.axis_index("col") * columns
    plane = group // 2
    origin = jnp.where(plane == 0, NONE, NEW)
    last = jnp.where(plane == 2, OLD, origin)
    once = jnp.ones_like(core)
    place = [
        jnp.stack([core, origin, lowest, shift, jnp.where(core == 0, LEAD, 1)]),
        jnp.stack([core, origin, lowest, shift, once]),
        jnp.stack([core, origin, lowest, shift, jnp.where(core == 0, 1, HOLD)]),
        jnp.stack([core, last, lowest, shift, once]),
        jnp.stack([1 - core, origin, lowest, shift, once]),
    ]
    place, factor_tiles = lax.optimization_barrier((place, factor_tiles))

    other_inverse = swap(diag_inverse[0])
    tables = (tile_rows, tile_cols, swap(tile_rows), swap(tile_cols))
    other_sources = swap(sources)
    other_factor = swap(factor_tiles[0])
    factor, inverse = prepare(factor_tiles[0], diag_inverse[0], other_factor, other_inverse)
    inputs = (sources, other_sources, inverse, factor)

    trades = [{0: 1, 1: 0, 2: 3, 3: 2}, {0: 3, 1: 2, 2: 1, 3: 0}, {0: 1, 1: 0, 2: 3, 3: 2}]
    arrived = jnp.zeros((1, columns, width, sources.shape[3]), F32)
    before = arrived
    planes = groups // 2
    for sweep in range(planes):
        sums, solved_even, _ = stage(place[sweep], tables, arrived, before, inputs, peers * columns)
        sums, solved_odd, leaving_even = stage(place[-1], tables, exchange(sums), None, inputs, peers * columns)
        leaving_odd = gather_sum(exchange(sums))
        if sweep < planes - 1:
            trade = trades[sweep]
            route = [(i, 2 * trade[i // 2] + i % 2) for i in range(groups)]
            before, arrived = arrived, lax.ppermute(leaving_odd, "chain", route)[None]

    first = core == 0
    even = jnp.stack([solved_even, leaving_even])
    odd = jnp.stack([solved_odd, leaving_odd])
    mine = jnp.where(first, even, odd)
    partner = swap(jnp.where(first, odd, even))
    whole = jnp.where(first, jnp.concatenate([mine, partner], 2), jnp.concatenate([partner, mine], 2))
    return (whole[0][None], whole[1][None])


def solution(mesh):
    return jax.shard_map(
        local,
        mesh=mesh,
        in_specs=(
            P("chain", "col", None, None),
            P("chain", "col", None, None),
            P("chain", "col", None, None),
            P("chain", "col"),
            P("chain", "col"),
        ),
        out_specs=(P("chain", "col", None, None), P("chain", "col", None, None)),
        check_vma=False,
    )
```

```python
import functools

import jax
import jax.numpy as jnp
from jax import lax
from jax.experimental import pallas as pl
from jax.experimental.pallas import tpu as pltpu
from jax.sharding import PartitionSpec as P

BF = jnp.bfloat16
F32 = jnp.float32
NONE, OLD, NEW = 0, 1, 2
LEAD, HOLD = 48, 50
VMEM = pl.BlockSpec(memory_space=pltpu.VMEM)
SMEM = pl.BlockSpec(memory_space=pltpu.SMEM)


def split(x):
    high = x.astype(BF)
    return high, (x - high.astype(F32)).astype(BF)


def left_side(x):
    high, low = split(x)
    return jnp.concatenate(
        [
            jnp.concatenate([high, high], 1),
            jnp.concatenate([low, jnp.zeros_like(low)], 1),
        ],
        0,
    )


def product(left, right):
    both = jnp.dot(left, right, preferred_element_type=F32)
    half = both.shape[0] // 2
    return both[:half] + both[half:]


def prepare_tile(tile, out_ref, at):
    high, low = split(tile.T)
    size = high.shape[0]
    out_ref[at, :size] = high
    out_ref[at, size:] = low


def prepare_tiles(tile_ref, out_ref, first, count):
    for i in range(count):
        prepare_tile(tile_ref[i], out_ref, first + i)


def prepare_own_body(tile_ref, inverse_ref, *refs):
    out_ref, out_inverse_ref = refs[-2:]
    prepare_tiles(tile_ref, out_ref, 0, tile_ref.shape[0])
    prepare_tiles(inverse_ref, out_inverse_ref, 0, inverse_ref.shape[0])


def prepare_shapes(own, own_inverse):
    size = own.shape[1]
    return tuple(jax.ShapeDtypeStruct((2 * x.shape[0], 2 * size, size), BF) for x in (own, own_inverse))


def prepare_own(own, own_inverse, sources, tables):
    return pl.pallas_call(
        prepare_own_body,
        out_shape=prepare_shapes(own, own_inverse),
        in_specs=[VMEM, VMEM, VMEM, SMEM, SMEM],
        out_specs=(VMEM, VMEM),
        compiler_params=pltpu.CompilerParams(vmem_limit_bytes=20 << 20),
        name="prepare_own",
    )(own, own_inverse, sources, *tables)


def gather_sum_body(arrived, total):
    for t in range(arrived.shape[1]):
        value = arrived[0, t]
        for j in range(1, arrived.shape[0]):
            value = value + arrived[j, t]
        total[t] = value


def gather_sum(arrived):
    return pl.pallas_call(
        gather_sum_body,
        out_shape=jax.ShapeDtypeStruct(arrived.shape[1:], F32),
        in_specs=[VMEM],
        out_specs=VMEM,
        compiler_params=pltpu.CompilerParams(vmem_limit_bytes=4 << 20),
        name="gather_sum",
    )(arrived)


def rates(place, k, rows, cols, other_rows, other_cols):
    other = place[0] > 0
    row = jnp.where(other, other_rows[0, k], rows[0, k])
    return row, jnp.where(other, other_cols[0, k], cols[0, k]) - place[3]


def clear(sums, times):
    if times is None:
        sums[...] = jnp.zeros_like(sums)
    else:

        @pl.loop(0, times)
        def _(_):
            sums[...] = jnp.zeros_like(sums)


def sources_of(place, t, width, source, other_source):
    here = pl.ds(pl.multiple_of(place[2], width), width)
    return jnp.where(place[0] > 0, other_source[0, t, here], source[0, t, here])


def opening_body(place, *refs):
    tables, refs = refs[:4], refs[4:]
    source, other_source, tile_ref, tile_inverse_ref, _, _, sums, factor, inverse, current = refs
    tiles, columns, width = tile_ref.shape[0], tile_inverse_ref.shape[0], sums.shape[1]
    prepare_tiles(tile_inverse_ref, inverse, columns, columns)
    clear(sums, place[4])
    for t in range(columns):
        right = sources_of(place, t, width, source, other_source)
        current[t] = left_side(product(left_side(right), inverse[place[0] * columns + t]))
    for k in range(tiles):
        prepare_tile(tile_ref[k], factor, tiles + k)
        row, col = rates(place, k, *tables)
        sums[row] += product(current[col], factor[place[0] * tiles + k])


def opening(place, tables, sources, other_sources, other, other_inverse, held, tile_rows):
    _, columns, width, size = sources.shape
    width = width // 2
    return pl.pallas_call(
        opening_body,
        out_shape=(jax.ShapeDtypeStruct((tile_rows, width, size), F32),) + prepare_shapes(other, other_inverse),
        in_specs=[SMEM] * 5 + [VMEM] * 6,
        out_specs=(VMEM,) * 3,
        scratch_shapes=[pltpu.VMEM((columns, 2 * width, 2 * size), BF)],
        input_output_aliases={9: 1, 10: 2},
        compiler_params=pltpu.CompilerParams(vmem_limit_bytes=20 << 20),
        name="opening",
    )(place, *tables, sources, other_sources, other, other_inverse, *held)


def stage_body(paced, place, *refs):
    tables, refs = refs[:4], refs[4:]
    arrived, refs = refs[0], refs[1:]
    before, refs = (refs[0], refs[1:]) if len(refs) == 9 else (None, refs)
    source, other_source, inverse, factor, sums, solved, inbound, current = refs
    tiles = factor.shape[0] // 2
    columns, width = inbound.shape[0], inbound.shape[1]
    clear(sums, place[4] if paced else None)
    for t in range(columns):
        total = arrived[0, t]
        for j in range(1, arrived.shape[0]):
            total = total + arrived[j, t]
        if before is not None:
            kept = jnp.where(place[1] == OLD, before[0, t], jnp.zeros_like(total))
            total = jnp.where(place[1] == NEW, total, kept)
        inbound[t] = total
        right = sources_of(place, t, width, source, other_source) - total
        value = product(left_side(right), inverse[place[0] * columns + t])
        solved[t] = value
        current[t] = left_side(value)
    for k in range(tiles):
        row, col = rates(place, k, *tables)
        sums[row] += product(current[col], factor[place[0] * tiles + k])


def stage(place, tables, arrivals, inputs, tile_rows, paced=False):
    small = jax.ShapeDtypeStruct(arrivals[0].shape[1:], F32)
    columns, width, size = small.shape
    return pl.pallas_call(
        functools.partial(stage_body, paced),
        out_shape=(jax.ShapeDtypeStruct((tile_rows, width, size), F32), small, small),
        in_specs=[SMEM] * 5 + [VMEM] * (len(arrivals) + 4),
        out_specs=[VMEM, VMEM, VMEM],
        scratch_shapes=[pltpu.VMEM((columns, 2 * width, 2 * size), BF)],
        compiler_params=pltpu.CompilerParams(vmem_limit_bytes=6 << 20),
        name="stage",
    )(place, *tables, *arrivals, *inputs)


def local(sources, diag_inverse, factor_tiles, tile_rows, tile_cols):
    group = lax.axis_index("chain")
    groups = lax.axis_size("chain")
    peers = lax.axis_size("col")
    core = group % 2
    columns = sources.shape[1]
    width = sources.shape[2] // 2

    def swap(x):
        return lax.ppermute(x, "chain", [(i, i ^ 1) for i in range(groups)])

    def exchange(x):
        return lax.all_to_all(x.reshape((peers, columns) + x.shape[1:]), "col", 0, 0)

    lowest = core * width
    shift = lax.axis_index("col") * columns
    plane = group // 2
    origin = jnp.where(plane == 0, NONE, NEW)
    last = jnp.where(plane == 2, OLD, origin)
    once = jnp.ones_like(core)
    place = [
        jnp.stack([core, origin, lowest, shift, jnp.where(core == 0, LEAD, 1)]),
        jnp.stack([core, origin, lowest, shift, once]),
        jnp.stack([core, origin, lowest, shift, jnp.where(core == 0, 1, HOLD)]),
        jnp.stack([core, last, lowest, shift, once]),
        jnp.stack([1 - core, origin, lowest, shift, once]),
    ]
    place, factor_tiles = lax.optimization_barrier((place, factor_tiles))

    other_inverse = swap(diag_inverse[0])
    tables = (tile_rows, tile_cols, swap(tile_rows), swap(tile_cols))
    other_sources = swap(sources)
    other_factor = swap(factor_tiles[0])
    held = prepare_own(factor_tiles[0], diag_inverse[0], sources, tables[:2])
    tile_total = peers * columns
    sums, factor, inverse = opening(
        place[0], tables, sources, other_sources, other_factor, other_inverse, held, tile_total
    )
    inputs = (sources, other_sources, inverse, factor)

    trades = [{0: 1, 1: 0, 2: 3, 3: 2}, {0: 3, 1: 2, 2: 1, 3: 0}, {0: 1, 1: 0, 2: 3, 3: 2}]
    arrived = before = None
    planes = groups // 2
    for sweep in range(planes):
        if sweep:
            arrivals = (arrived, arrived if before is None else before)
            sums, solved_even, _ = stage(place[sweep], tables, arrivals, inputs, tile_total, paced=sweep == 2)
        sums, solved_odd, leaving_even = stage(place[-1], tables, (exchange(sums),), inputs, tile_total)
        leaving_odd = gather_sum(exchange(sums))
        if sweep < planes - 1:
            trade = trades[sweep]
            route = [(i, 2 * trade[i // 2] + i % 2) for i in range(groups)]
            before, arrived = arrived, lax.ppermute(leaving_odd, "chain", route)[None]

    first = core == 0
    even = jnp.stack([solved_even, leaving_even])
    odd = jnp.stack([solved_odd, leaving_odd])
    mine = jnp.where(first, even, odd)
    partner = swap(jnp.where(first, odd, even))
    whole = jnp.where(first, jnp.concatenate([mine, partner], 2), jnp.concatenate([partner, mine], 2))
    return (whole[0][None], whole[1][None])


def solution(mesh):
    return jax.shard_map(
        local,
        mesh=mesh,
        in_specs=(
            P("chain", "col", None, None),
            P("chain", "col", None, None),
            P("chain", "col", None, None),
            P("chain", "col"),
            P("chain", "col"),
        ),
        out_specs=(P("chain", "col", None, None), P("chain", "col", None, None)),
        check_vma=False,
    )
```
